32 devices in a mesh: groups: 2 (over x), seq: 16 (over z, y, core).
Axes of the slice: x: 2, y: 2, z: 4, core: 2. Of those that a mesh axis runs over, the one named last changes fastest.
Arguments:
- queries: bfloat16 [8192, 1024], P(('groups', 'seq')), parts along dimension 0, may hold values from -6 to 6
- keys: bfloat16 [8192, 1024], P(('groups', 'seq')), parts along dimension 0, may hold values from -6 to 6
- values: bfloat16 [8192, 1024], P(('groups', 'seq')), parts along dimension 0, may hold values from -6 to 6
- out_grad: bfloat16 [8192, 1024], P(('groups', 'seq')), parts along dimension 0, may hold values from -0.09375 to 0.09375
- maps: float32 [2, 8, 128, 128], replicated, may hold values from -0.5 to 0.5
- gain: bfloat16 [1024], replicated, may hold values from 0.25 to 1.75
- first_moment: float32 [2048, 128], P('seq'), may hold values from -1.8 to 1.8
- second_moment: float32 [2048, 128], P('seq'), may hold values from 0.01 to 0.3
Outputs:
- attention: bfloat16 [8192, 1024], P(('groups', 'seq')), parts along dimension 0
- new_maps: float32 [4, 8, 128, 128], P('groups'), parts along dimension 0
- new_moments: float32 [4, 2048, 128], P('groups', 'seq'), parts along dimension 0
The draws below stay inside these ranges and needn't reach their ends.
There are 2 independent parts, one for each index of `groups`. The reference program is written for one: setup_inputs(seed, part) draws one part's arguments, and reference() takes and returns one part's arrays. A program takes and returns all parts, laid end to end along the dimension named above; an argument that names none is the same for every part. Nothing has to cross between parts.
All inputs are finite; a program needn't handle non-finite values.
Results may differ from the reference program's by a relative error of at most 0.0057.
Values sent between devices are 32-bit elements; how exact they have to be, the bound alone decides.
No kernel may reach another device: no remote copies, remote signals or barrier semaphores. Data moves between devices by JAX's collectives and lax.ppermute only.
A program may use at most 320 MiB of HBM per device.

```python
import math
import jax
import jax.numpy as jnp
from jax import lax

H = 8
E = 128
TOK_DEV = 256
SPAN = 256
OPT_STEP = 10
TOKENS = 4096
N_SEQ = 16


def block_levels(own_key, extent, cuts, least, top_value):
    factor_of, own = 1.0, jax.random.fold_in(own_key, 6)
    for dim, blocks in cuts:
        draws = jnp.exp(jax.random.uniform(jax.random.fold_in(own, dim), (blocks,), jnp.float32, least / len(cuts), top_value / len(cuts)))
        factor_of = factor_of * jnp.repeat(draws, extent[dim] // blocks).reshape([-1 if axis == dim else 1 for axis in range(len(extent))])
    return factor_of


def scatter_about(rng, shape, deviation, most, cuts=(), kind=jnp.bfloat16):
    result = deviation * jax.random.normal(rng, shape, jnp.float32)
    if cuts:
        result = result * block_levels(rng, shape, cuts, -0.22, 0.18)
    return jnp.clip(result, -most, most).astype(kind)


def setup_inputs(seed: int = 0, part: int = 0) -> dict:
    key_list = jax.random.split(jax.random.key(seed), 9)
    own_keys = jax.random.split(jax.random.fold_in(key_list[8], part), 9)
    queries = scatter_about(own_keys[0], (TOKENS, H * E), 1.0, 6.0, ((0, 16),))
    keys = scatter_about(own_keys[1], (TOKENS, H * E), 1.0, 6.0, ((0, 16),))
    values = scatter_about(own_keys[2], (TOKENS, H * E), 1.0, 6.0, ((0, 16),))
    out_grad = scatter_about(own_keys[3], (TOKENS, H * E), (1.0 / (TOK_DEV * N_SEQ) ** 0.5), 0.09375, ((0, 16),))
    maps = scatter_about(key_list[4], (2, H, E, E), E ** -0.5, 0.5, (), jnp.float32)
    gain = jnp.clip(1.0 + 0.15 * jax.random.normal(key_list[5], (H * E,), jnp.float32), 0.25, 1.75).astype(jnp.bfloat16)
    first_moment = scatter_about(key_list[6], (2 * H * E, E), 0.3, 1.8, ((0, 16),), jnp.float32)
    second_moment = jnp.clip(jnp.exp(math.log(0.3) - 3.4011974 * jax.random.uniform(key_list[7], (2 * H * E, E), jnp.float32) ** block_levels(key_list[7], (2 * H * E, E), ((0, 16),), -0.2, 0.2)), 0.01, 0.3)
    return dict(queries=queries, keys=keys, values=values, out_grad=out_grad, maps=maps, gain=gain, first_moment=first_moment, second_moment=second_moment)


BETA_ONE = 0.9
BETA_TWO = 0.95
RATE = 0.01
TINY = 1e-08
NORM_EPS = 1e-06

def widen(tensor):
    return tensor.astype(jnp.float32)

def causal(length):
    places = jnp.arange(length)
    return places[:, None] >= places[None, :]

def silu_slope(preact):
    sigmoid = jax.nn.sigmoid(preact)
    return sigmoid * (1.0 + preact * (1.0 - sigmoid))

def adam_rows(gradient, weights, first_old, second_old):
    first_new = BETA_ONE * first_old + (1.0 - BETA_ONE) * gradient
    second_new = BETA_TWO * second_old + (1.0 - BETA_TWO) * gradient * gradient
    first_hat = first_new / (1.0 - BETA_ONE ** OPT_STEP)
    second_hat = second_new / (1.0 - BETA_TWO ** OPT_STEP)
    return (weights - RATE * first_hat / (jnp.sqrt(second_hat) + TINY), first_new, second_new)

def head_pass(pieces):
    query_in, key_in, value_in, grad_in, map_pair, gain_head = pieces
    low_maps = map_pair.astype(jnp.bfloat16)
    pre_query = jnp.einsum('nche,hef->nchf', widen(query_in), widen(low_maps[0]))
    pre_key = jnp.einsum('nche,hef->nchf', widen(key_in), widen(low_maps[1]))
    feat_query = jax.nn.silu(pre_query).astype(jnp.bfloat16)
    feat_key = jax.nn.silu(pre_key).astype(jnp.bfloat16)
    own_states = jnp.einsum('ncht,ncho->nhto', widen(feat_key), widen(value_in))
    before = (jnp.cumsum(own_states, 0) - own_states).astype(jnp.bfloat16)
    masked = causal(SPAN)[None, None]
    inter = jnp.einsum('ncht,nhto->ncho', widen(feat_query), widen(before))
    scores = jnp.einsum('ncht,nsht->nhcs', widen(feat_query), widen(feat_key))
    scores = jnp.where(masked, scores, 0.0).astype(jnp.bfloat16)
    intra = jnp.einsum('nhcs,nsho->ncho', widen(scores), widen(value_in))
    raw = inter + intra
    scale = lax.rsqrt(lax.optimization_barrier(jnp.mean(raw * raw, -1, keepdims=True)) + NORM_EPS)
    unit = raw * scale
    gain_wide = widen(gain_head)
    output = (unit * gain_wide).astype(jnp.bfloat16)
    dunit = widen(grad_in) * gain_wide
    grad_raw = (scale * (dunit - unit * lax.optimization_barrier(jnp.mean(dunit * unit, -1, keepdims=True)))).astype(jnp.bfloat16)
    grad_states = jnp.einsum('ncht,ncho->nhto', widen(feat_query), widen(grad_raw))
    after = (lax.optimization_barrier(jnp.sum(grad_states, 0))[None] - jnp.cumsum(grad_states, 0)).astype(jnp.bfloat16)
    pscores = jnp.einsum('ncho,nsho->nhcs', widen(grad_raw), widen(value_in))
    pscores = jnp.where(masked, pscores, 0.0).astype(jnp.bfloat16)
    grad_fq = jnp.einsum('ncho,nhto->ncht', widen(grad_raw), widen(before))
    grad_fq = grad_fq + jnp.einsum('nhcs,nsht->ncht', widen(pscores), widen(feat_key))
    grad_fk = jnp.einsum('ncho,nhto->ncht', widen(value_in), widen(after))
    grad_fk = grad_fk + jnp.einsum('nhcs,ncht->nsht', widen(pscores), widen(feat_query))
    grad_pq = (grad_fq * silu_slope(pre_query)).astype(jnp.bfloat16)
    grad_pk = (grad_fk * silu_slope(pre_key)).astype(jnp.bfloat16)
    grad_query = jnp.einsum('ncht,nchu->htu', widen(query_in), widen(grad_pq))
    grad_key = jnp.einsum('ncht,nchu->htu', widen(key_in), widen(grad_pk))
    return (output, jnp.stack([grad_query, grad_key]))

def reference(queries, keys, values, out_grad, maps, gain, first_moment, second_moment):
    total = queries.shape[0]
    blocks = total // SPAN

    def arrange(tensor):
        return tensor.reshape(blocks, SPAN, H, E).transpose(2, 0, 1, 3)[:, :, :, None, :]
    pieces = (arrange(queries), arrange(keys), arrange(values), arrange(out_grad), maps.transpose(1, 0, 2, 3)[:, :, None], gain.reshape(H, 1, E))
    outputs, grads = lax.map(head_pass, pieces)
    attention = outputs[:, :, :, 0, :].transpose(1, 2, 0, 3).reshape(total, H * E)
    gradient = grads[:, :, 0].transpose(1, 0, 2, 3).reshape(2 * H * E, E)
    new_rows, first_new, second_new = adam_rows(gradient, maps.reshape(2 * H * E, E), first_moment, second_moment)
    return (attention, new_rows.reshape(2, H, E, E), jnp.stack([first_new, second_new]))
```

```python
import jax
import jax.numpy as jnp
from jax import lax
from jax.sharding import PartitionSpec as P

H = 8
E = 128
SPAN = 256
OPT_STEP = 10


BETA_ONE = 0.9
BETA_TWO = 0.95
RATE = 0.01
TINY = 1e-08
NORM_EPS = 1e-06


def masks_of(count):
    masks, step = [], 1
    while step < count:
        masks.append(step if step != 8 else 12)
        step *= 2
    return masks


def swap(value, mask):
    count = lax.axis_size("seq")
    return lax.ppermute(value, "seq", [(i, i ^ mask) for i in range(count)])


def send_up(value, mask, bit, upward):
    count = lax.axis_size("seq")
    pairs = [(i, i ^ mask) for i in range(count) if bool(i & bit) != upward]
    return lax.ppermute(value, "seq", pairs)


def part(value, index):
    half = value.shape[0] // 2
    return lax.dynamic_slice_in_dim(value, index * half, half, 0)


def scan_states(own, upward):
    count = lax.axis_size("seq")
    masks = masks_of(count)
    me = lax.axis_index("seq")
    spread = min(2, len(masks))
    held, kept = own, []
    for level in range(spread):
        bit = (me >> level) & 1
        got = swap(part(held, 1 - bit), masks[level])
        mine = part(held, bit)
        receiver = (bit == 1) if upward else (bit == 0)
        kept.append((bit, receiver, jnp.where(receiver, got, mine)))
        held = mine + got
    before = None
    for level in range(spread, len(masks)):
        last = level == len(masks) - 1
        bit = (me >> level) & 1
        receiver = (bit == 1) if upward else (bit == 0)
        if last:
            got = send_up(held, masks[level], 1 << level, upward)
        else:
            got = swap(held, masks[level])
            held_next = held + got
        gain = jnp.where(receiver, got, 0.0)
        before = gain if before is None else before + gain
        if not last:
            held = held_next
    if before is None:
        before = jnp.zeros_like(held)
    for level in reversed(range(spread)):
        bit, receiver, lower = kept[level]
        mine = before + jnp.where(receiver, lower, 0.0)
        theirs = before + jnp.where(receiver, 0.0, lower)
        got = swap(theirs, masks[level])
        before = jnp.where(bit == 0, jnp.concatenate([mine, got]), jnp.concatenate([got, mine]))
    return before


def relative_order(count):
    masks = masks_of(count)
    order = [0]
    for mask in reversed(masks):
        order = order + [i ^ mask for i in order]
    return order


def scatter_rows(rows):
    count = lax.axis_size("seq")
    masks = masks_of(count)
    me = lax.axis_index("seq")
    blocks = rows.reshape(count, -1, E)
    held = jnp.take(blocks, jnp.asarray(relative_order(count), jnp.int32) ^ me, axis=0)
    for mask in masks:
        half = held.shape[0] // 2
        held = held[:half] + swap(held[half:], mask)
    return held[0]


def gather_rows(own):
    count = lax.axis_size("seq")
    masks = masks_of(count)
    me = lax.axis_index("seq")
    held = own[None]
    for mask in reversed(masks):
        held = jnp.concatenate([held, swap(held, mask)])
    order = relative_order(count)
    back = [order.index(i) for i in range(count)]
    table = jnp.asarray(back, jnp.int32)
    return jnp.take(held, jnp.take(table, jnp.arange(count) ^ me), axis=0).reshape(-1, E)


def silu_slope(preact):
    sigmoid = jax.nn.sigmoid(preact)
    return sigmoid * (1.0 + preact * (1.0 - sigmoid))


def adam_rows(gradient, weights, first_old, second_old):
    first_new = BETA_ONE * first_old + (1.0 - BETA_ONE) * gradient
    second_new = BETA_TWO * second_old + (1.0 - BETA_TWO) * gradient * gradient
    first_hat = first_new / (1.0 - BETA_ONE**OPT_STEP)
    second_hat = second_new / (1.0 - BETA_TWO**OPT_STEP)
    return (weights - RATE * first_hat / (jnp.sqrt(second_hat) + TINY), first_new, second_new)


def product(form, left, right):
    return jnp.einsum(form, left, right, preferred_element_type=jnp.float32)


def local(queries, keys, values, out_grad, maps, gain, first_moment, second_moment):
    tok_rows = queries.shape[0]
    blocks = tok_rows // SPAN

    def arrange(tensor):
        return tensor.reshape(blocks, SPAN, H, E)

    query_in = arrange(queries)
    key_in = arrange(keys)
    value_in = arrange(values)
    grad_in = arrange(out_grad)
    low_maps = maps.astype(jnp.bfloat16)
    pre_query = product("nche,hef->nchf", query_in, low_maps[0])
    pre_key = product("nche,hef->nchf", key_in, low_maps[1])
    feat_query = jax.nn.silu(pre_query).astype(jnp.bfloat16)
    feat_key = jax.nn.silu(pre_key).astype(jnp.bfloat16)
    own_states = product("ncht,ncho->nhto", feat_key, value_in)
    start_state = scan_states(jnp.sum(own_states, 0), True)
    places = jnp.arange(SPAN)
    masked = (places[:, None] >= places[None, :])[None, None]
    scores = jnp.where(masked, product("ncht,nsht->nhcs", feat_query, feat_key), 0.0).astype(
        jnp.bfloat16
    )
    intra = product("nhcs,nsho->ncho", scores, value_in)
    before = (start_state[None] + jnp.cumsum(own_states, 0) - own_states).astype(jnp.bfloat16)
    raw = product("ncht,nhto->ncho", feat_query, before) + intra
    scale = lax.rsqrt(jnp.mean(raw * raw, -1, keepdims=True) + NORM_EPS)
    unit = raw * scale
    gain_wide = gain.reshape(H, E).astype(jnp.float32)
    attention = (unit * gain_wide).astype(jnp.bfloat16).reshape(tok_rows, H * E)
    dunit = grad_in.astype(jnp.float32) * gain_wide
    grad_raw = (scale * (dunit - unit * jnp.mean(dunit * unit, -1, keepdims=True))).astype(
        jnp.bfloat16
    )
    grad_states = product("ncht,ncho->nhto", feat_query, grad_raw)
    after_state = scan_states(jnp.sum(grad_states, 0), False)
    pscores = jnp.where(masked, product("ncho,nsho->nhcs", grad_raw, value_in), 0.0).astype(
        jnp.bfloat16
    )
    grad_fq = product("ncho,nhto->ncht", grad_raw, before) + product(
        "nhcs,nsht->ncht", pscores, feat_key
    )
    local_fk = product("nhcs,ncht->nsht", pscores, feat_query)
    after = (after_state[None] + jnp.sum(grad_states, 0)[None] - jnp.cumsum(grad_states, 0)).astype(
        jnp.bfloat16
    )
    grad_fk = product("ncho,nhto->ncht", value_in, after) + local_fk
    grad_pq = (grad_fq * silu_slope(pre_query)).astype(jnp.bfloat16)
    grad_pk = (grad_fk * silu_slope(pre_key)).astype(jnp.bfloat16)
    grad_query = product("ncht,nchu->htu", query_in, grad_pq)
    grad_key = product("ncht,nchu->htu", key_in, grad_pk)
    local_grad = jnp.stack([grad_query, grad_key]).reshape(2 * H * E, E)
    share = 2 * H * E // lax.axis_size("seq")
    offset = lax.axis_index("seq") * share
    flat_maps = maps.reshape(2 * H * E, E)
    own_grad = scatter_rows(local_grad)
    own_maps = lax.dynamic_slice_in_dim(flat_maps, offset, share, 0)
    new_part, first_new, second_new = adam_rows(own_grad, own_maps, first_moment, second_moment)
    new_flat = gather_rows(new_part)
    new_maps = new_flat.reshape(2, H, E, E)
    return (attention, new_maps, jnp.stack([first_new, second_new]))


def solution(mesh):
    in_specs = (
        P(("groups", "seq"), None),
        P(("groups", "seq"), None),
        P(("groups", "seq"), None),
        P(("groups", "seq"), None),
        P(),
        P(),
        P("seq", None),
        P("seq", None),
    )
    out_specs = (
        P(("groups", "seq"), None),
        P("groups", None, None, None),
        P("groups", "seq", None),
    )
    return jax.shard_map(local, mesh=mesh, in_specs=in_specs, out_specs=out_specs, check_vma=False)
```

```python
import jax
import jax.numpy as jnp
from jax import lax
from jax.experimental import pallas as pl
from jax.experimental.pallas import tpu as pltpu
from jax.sharding import PartitionSpec as P

H = 8
E = 128
SPAN = 256
OPT_STEP = 10


BETA_ONE = 0.9
BETA_TWO = 0.95
RATE = 0.01
TINY = 1e-08
NORM_EPS = 1e-06

VMEM = pl.BlockSpec(memory_space=pltpu.VMEM)
SMEM = pl.BlockSpec(memory_space=pltpu.SMEM)


def masks_of(count):
    masks, step = [], 1
    while step < count:
        masks.append(step if step != 8 else 12)
        step *= 2
    return masks


def swap(value, mask):
    count = lax.axis_size("seq")
    return lax.ppermute(value, "seq", [(i, i ^ mask) for i in range(count)])


def bits_of():
    count = lax.axis_size("seq")
    me = lax.axis_index("seq")
    return [(me >> level) & 1 for level in range(len(masks_of(count)))]


def scan_states(mine, theirs, upward):
    masks, bits = masks_of(lax.axis_size("seq")), bits_of()
    takes = [(bit == 1) if upward else (bit == 0) for bit in bits]

    got = swap(theirs, masks[0])
    chip_other = jnp.where(takes[0], got, mine)
    held = mine + got
    got = swap(held[2:], masks[1])
    pair_other = jnp.where(takes[1], got, held[:2])
    held = held[:2] + got
    before = None
    for level in range(2, len(masks)):
        got = swap(held, masks[level])
        share = jnp.where(takes[level], got, 0.0)
        before = share if before is None else before + share
        held = held + got
    own = before + jnp.where(takes[1], pair_other, 0.0)
    got = swap(before + jnp.where(takes[1], 0.0, pair_other), masks[1])
    base = jnp.concatenate([own, got])
    own = base + jnp.where(takes[0], chip_other, 0.0)
    return own, swap(base + jnp.where(takes[0], 0.0, chip_other), masks[0])


def reduce_quarter(mine, theirs):
    masks = masks_of(lax.axis_size("seq"))
    held = mine + swap(theirs, masks[0])
    deep = held.shape[0] // 2
    held = held[:deep] + swap(held[deep:], masks[1])
    for mask in masks[2:]:
        held = held + swap(held, mask)
    return held


def spread_quarter(quarter):
    masks = masks_of(lax.axis_size("seq"))
    held = jnp.concatenate([quarter, swap(quarter, masks[1])])
    return held, swap(held, masks[0])


def gather_upper(own):
    masks, bits = masks_of(lax.axis_size("seq")), bits_of()
    held = own[None]
    for level in range(2, len(masks)):
        got = swap(held, masks[level])
        held = jnp.where(
            bits[level] == 0, jnp.concatenate([held, got]), jnp.concatenate([got, held])
        )
    return held


def silu_slope(preact):
    sigmoid = jax.nn.sigmoid(preact)
    return sigmoid * (1.0 + preact * (1.0 - sigmoid))


def adam_rows(gradient, weights, first_old, second_old):
    first_new = BETA_ONE * first_old + (1.0 - BETA_ONE) * gradient
    second_new = BETA_TWO * second_old + (1.0 - BETA_TWO) * gradient * gradient
    first_hat = first_new / (1.0 - BETA_ONE**OPT_STEP)
    second_hat = second_new / (1.0 - BETA_TWO**OPT_STEP)
    return (weights - RATE * first_hat / (jnp.sqrt(second_hat) + TINY), first_new, second_new)


def nn(left, right):
    return lax.dot_general(left, right, (((1,), (0,)), ((), ())), preferred_element_type=jnp.float32)


def nt(left, right):
    return lax.dot_general(left, right, (((1,), (1,)), ((), ())), preferred_element_type=jnp.float32)


def tn(left, right):
    return lax.dot_general(left, right, (((0,), (0,)), ((), ())), preferred_element_type=jnp.float32)


def low(value):
    return value.astype(jnp.bfloat16)


def causal():
    rows = lax.broadcasted_iota(jnp.int32, (SPAN, SPAN), 0)
    return rows >= lax.broadcasted_iota(jnp.int32, (SPAN, SPAN), 1)


def related(place_ref):
    core, pair = place_ref[0], place_ref[1]
    for spot in range(H):
        far_core, far_pair, deep = spot >> 2, (spot >> 1) & 1, spot & 1
        head = deep * 4 + (1 - pair if far_pair else pair) * 2 + (1 - core if far_core else core)
        yield far_core, spot & 3, head, pl.ds(pl.multiple_of(head * E, E), E)


def key_kernel(place_ref, key_ref, value_ref, map_ref, feat_ref, mine_ref, theirs_ref):
    for half, spot, head, cols in related(place_ref):
        feat = low(jax.nn.silu(nn(key_ref[:, cols], low(map_ref[1, head]))))
        feat_ref[:, cols] = feat
        (mine_ref, theirs_ref)[half][spot] = tn(feat, value_ref[:, cols])


def query_kernel(
    query_ref, key_ref, value_ref, feat_key_ref, map_ref,
    feat_ref, slope_ref, key_slope_ref, intra_ref,
):
    masked = causal()
    for head in range(H):
        cols = slice(head * E, head * E + E)
        pre = nn(query_ref[:, cols], low(map_ref[0, head]))
        feat = low(jax.nn.silu(pre))
        feat_ref[:, cols] = feat
        slope_ref[:, cols] = silu_slope(pre)
        scores = low(jnp.where(masked, nt(feat, feat_key_ref[:, cols]), 0.0))
        intra_ref[:, cols] = nn(scores, value_ref[:, cols])
        key_slope_ref[:, cols] = silu_slope(nn(key_ref[:, cols], low(map_ref[1, head])))


def norm_kernel(
    place_ref, near_ref, far_ref, feat_ref, intra_ref, grad_ref, gain_ref,
    out_ref, grad_raw_ref, mine_ref, theirs_ref,
):
    for half, spot, head, cols in related(place_ref):
        before = low((near_ref, far_ref)[half][spot])
        feat = feat_ref[:, cols]
        raw = nn(feat, before) + intra_ref[:, cols]
        scale = lax.rsqrt(jnp.mean(raw * raw, -1, keepdims=True) + NORM_EPS)
        unit = raw * scale
        gain = gain_ref[:, cols].astype(jnp.float32)
        out_ref[:, cols] = low(unit * gain)
        dunit = grad_ref[:, cols].astype(jnp.float32) * gain
        grad_raw = low(scale * (dunit - unit * jnp.mean(dunit * unit, -1, keepdims=True)))
        grad_raw_ref[:, cols] = grad_raw
        (mine_ref, theirs_ref)[half][spot] = tn(feat, grad_raw)


def back_kernel(
    place_ref, near_ref, far_ref, grad_raw_ref, value_ref, feat_key_ref, feat_ref, slope_ref,
    query_ref, local_ref, mine_ref, theirs_ref,
):
    masked = causal()
    for half, spot, head, cols in related(place_ref):
        before = low((near_ref, far_ref)[half][spot])
        grad_raw = grad_raw_ref[:, cols]
        pscores = low(jnp.where(masked, nt(grad_raw, value_ref[:, cols]), 0.0))
        grad_feat = nt(grad_raw, before) + nn(pscores, feat_key_ref[:, cols])
        (mine_ref, theirs_ref)[half][spot] = tn(
            query_ref[:, cols], low(grad_feat * slope_ref[:, cols])
        )
        local_ref[:, cols] = tn(pscores, feat_ref[:, cols])


def last_kernel(
    place_ref, near_ref, far_ref, value_ref, local_ref, slope_ref, key_ref, mine_ref, theirs_ref
):
    for half, spot, head, cols in related(place_ref):
        after = low((near_ref, far_ref)[half][spot])
        grad_feat = nt(value_ref[:, cols], after) + local_ref[:, cols]
        (mine_ref, theirs_ref)[half][spot] = tn(
            key_ref[:, cols], low(grad_feat * slope_ref[:, cols])
        )


def lay_kernel(place_ref, near_q, far_q, near_k, far_k, out_ref):
    core, pair = place_ref[0], place_ref[1]
    deep = out_ref.shape[1]
    for index, halves in enumerate(((near_q, far_q), (near_k, far_k))):
        for far_core in range(2):
            for far_pair in range(2):
                spot = (1 - pair if far_pair else pair) * 2 + (1 - core if far_core else core)
                block = halves[far_core][far_pair * deep : far_pair * deep + deep]
                out_ref[index, :, spot] = block


def kernel_call(body, outs, products, *arrays):
    size = sum(a.size * a.dtype.itemsize for a in arrays) + sum(o.size * o.dtype.itemsize for o in outs)
    return pl.pallas_call(
        body,
        out_shape=outs,
        in_specs=[SMEM if a.dtype == jnp.int32 else VMEM for a in arrays],
        out_specs=[VMEM] * len(outs),
        cost_estimate=pl.CostEstimate(
            flops=products * H * 2 * SPAN * E * E, bytes_accessed=size, transcendentals=0
        ),
        name=body.__name__,
    )(*arrays)


def local(queries, keys, values, out_grad, maps, gain, first_moment, second_moment):
    count = lax.axis_size("seq")
    me = lax.axis_index("seq")
    share = 2 * H * E // count
    deep = count // 8
    core, pair, quarter, upper = me & 1, (me >> 1) & 1, me & 3, me >> 2
    place = jnp.stack([core, pair]).astype(jnp.int32)
    wide = jax.ShapeDtypeStruct((SPAN, H * E), jnp.bfloat16)
    full = jax.ShapeDtypeStruct((SPAN, H * E), jnp.float32)
    some = jax.ShapeDtypeStruct((H // 2, E, E), jnp.float32)

    feat_key, mine, theirs = kernel_call(
        key_kernel, [wide, some, some], 2, place, keys, values, maps
    )
    near, far = scan_states(mine, theirs, True)
    feat_query, slope_query, slope_key, intra = kernel_call(
        query_kernel, [wide, full, full, full], 6, queries, keys, values, feat_key, maps
    )
    attention, grad_raw, mine, theirs = kernel_call(
        norm_kernel, [wide, wide, some, some], 2,
        place, near, far, feat_query, intra, out_grad, gain.reshape(1, H * E),
    )
    after_near, after_far = scan_states(mine, theirs, False)
    local_fk, mine_q, theirs_q = kernel_call(
        back_kernel, [full, some, some], 8,
        place, near, far, grad_raw, values, feat_key, feat_query, slope_query, queries,
    )
    mine_k, theirs_k = kernel_call(
        last_kernel, [some, some], 2,
        place, after_near, after_far, values, local_fk, slope_key, keys,
    )

    moments = gather_upper(jnp.stack([first_moment, second_moment]))
    moments = moments.reshape(2, deep, 2, share, E)
    halves = maps.reshape(2, deep, 4, share, E)
    old = lax.dynamic_index_in_dim(halves, quarter, 2, keepdims=False)
    pieces, own_grads = [], []
    for half, (mine, theirs) in enumerate(((mine_q, theirs_q), (mine_k, theirs_k))):
        if share != E:
            mine, theirs = by_share(mine, theirs, core, pair, deep, share)
        total = reduce_quarter(mine, theirs)
        fresh, _, _ = adam_rows(total, old[half], moments[half, :, 0], moments[half, :, 1])
        pieces += spread_quarter(fresh)
        own_grads.append(lax.dynamic_index_in_dim(total, upper % deep, 0, keepdims=False))
    own_grad = jnp.where(upper < deep, own_grads[0], own_grads[1])
    _, first_new, second_new = adam_rows(own_grad, own_grad, first_moment, second_moment)
    (new_maps,) = kernel_call(
        lay_kernel, [jax.ShapeDtypeStruct((2, deep, 4, share, E), jnp.float32)], 0, place, *pieces
    )
    return (attention, new_maps.reshape(2, H, E, E), jnp.stack([first_new, second_new]))


def by_share(mine, theirs, core, pair, deep, share):
    both = jnp.concatenate([mine, theirs]).reshape(2, 2, 2, E, E)
    both = jnp.where(core == 0, both, both[::-1])
    both = jnp.where(pair == 0, both, both[:, ::-1])
    both = both.transpose(2, 1, 0, 3, 4).reshape(deep, 2, 2, share, E).transpose(2, 1, 0, 3, 4)
    both = jnp.where(core == 0, both, both[::-1])
    both = jnp.where(pair == 0, both, both[:, ::-1])
    return both.reshape(2, 2 * deep, share, E)


def solution(mesh):
    in_specs = (
        P(("groups", "seq"), None),
        P(("groups", "seq"), None),
        P(("groups", "seq"), None),
        P(("groups", "seq"), None),
        P(),
        P(),
        P("seq", None),
        P("seq", None),
    )
    out_specs = (
        P(("groups", "seq"), None),
        P("groups", None, None, None),
        P("groups", "seq", None),
    )
    return jax.shard_map(local, mesh=mesh, in_specs=in_specs, out_specs=out_specs, check_vma=False)
```
